32 devices in a mesh: cfg: 2 (over x), space: 16 (over z, y, core).
Axes of the slice: x: 2, y: 2, z: 4, core: 2. Of those that a mesh axis runs over, the one named last changes fastest.
Arguments:
- eigenvectors: bfloat16 [8, 2, 3, 128, 16, 1024], P('cfg', None, None, None, 'space'), parts along dimension 0, may hold values from -3 to 3
- link_field: bfloat16 [8, 3, 2, 3, 3, 16, 1024], P('cfg', None, None, None, None, 'space'), parts along dimension 0, may hold values from -2.5 to 2.5
- momentum: int32 [3], replicated, may hold values from -2 to 2
- directions: int32 [4], replicated, may hold values from 0 to 2, as said below
- offsets: int32 [4], replicated, may hold values from 0 to 124
Outputs:
- elementals: float32 [8, 2, 4, 128, 128], P('cfg', None, None, 'space'), parts along dimension 0
The draws below stay inside these ranges and needn't reach their ends.
There are 2 independent parts, one for each index of `cfg`. The reference program is written for one: setup_inputs(seed, part) draws one part's arguments, and reference() takes and returns one part's arrays. A program takes and returns all parts, laid end to end along the dimension named above; an argument that names none is the same for every part. Nothing has to cross between parts.
Inputs may be any that keep to these rules, and one draw needn't show every extreme that they name: `directions`: exactly 2 of the timeslices have direction 0 (the first dimension); each other one has direction 1 or 2.
All inputs are finite; a program needn't handle non-finite values.
Results may differ from the reference program's by a relative error of at most 0.0041.
Values may be sent and summed in bfloat16 or wider, within the bound.
No kernel may reach another device: no remote copies, remote signals or barrier semaphores. Data moves between devices by JAX's collectives and lax.ppermute only.
A program may use at most 128 MiB of HBM per device.

```python
import math
import jax
import jax.numpy as jnp
from jax import lax

NEV = 128
BLK = 4
TSL = 4
LY = 32
LZ = 32
LX = 16
LYZ = 1024


def draw_directions(key, part):
    ranking = jax.random.permutation(jax.random.fold_in(key, 17), TSL)
    return jnp.where(ranking < TSL // 2, 0, 1 + ranking % 2).astype(jnp.int32)


def place_ends(values, own_key, least, top_value):
    longest = values.shape.index(max(values.shape))
    spots = []
    for shift in (0, 1):
        where = [jax.random.randint(jax.random.fold_in(own_key, axis), (), 0, length) for axis, length in enumerate(values.shape)]
        where[longest] = (where[longest] + shift) % values.shape[longest]
        spots.append(tuple(where))
    return values.at[spots[0]].set(least).at[spots[1]].set(top_value)


def levels(key, shape, split, least, largest):
    def one(axis_at, parts):
        steps = jax.random.uniform(jax.random.fold_in(jax.random.fold_in(key, 6), axis_at), (parts,), jnp.float32, least / len(split), largest / len(split))
        return jnp.repeat(jnp.exp(steps), shape[axis_at] // parts).reshape((-1,) + (1,) * (len(shape) - axis_at - 1))

    gain = one(*split[0])
    for cut in split[1:]:
        gain = gain * one(*cut)
    return gain


def normal_values(rng, shape, spread, bound, cuts=(), kind=jnp.bfloat16):
    values = spread * jax.random.normal(rng, shape, jnp.float32)
    if cuts:
        values = values * levels(rng, shape, cuts, -0.22, 0.18)
    return jnp.clip(values, -bound, bound).astype(kind)


def setup_inputs(seed: int = 0, part: int = 0) -> dict:
    streams_of = jax.random.split(jax.random.key(seed), 6)
    own_keys = jax.random.split(jax.random.fold_in(streams_of[5], part), 6)
    return {
        "eigenvectors": normal_values(own_keys[0], (TSL, 2, 3, NEV, LX, LYZ), 0.5, 3.0, ((4, 16),)),
        "link_field": normal_values(own_keys[1], (TSL, 3, 2, 3, 3, LX, LYZ), 6 ** -0.5, 2.5, ((5, 16),)),
        "momentum": jax.random.randint(streams_of[2], (3,), -2, 3).astype(jnp.int32),
        "directions": draw_directions(jax.random.fold_in(streams_of[5], 71), part),
        "offsets": place_ends(jax.random.randint(streams_of[4], (TSL,), 0, NEV - BLK + 1), jax.random.fold_in(streams_of[4], 1), 0, NEV - BLK).astype(jnp.int32),
    }


epsilon_cycles = ((0, 1, 2), (1, 2, 0), (2, 0, 1))

def phase_table(momentum, x_sites, extent):
    y_sites = jnp.arange(LY, dtype=jnp.int32)
    z_sites = jnp.arange(LZ, dtype=jnp.int32)
    x_turns = (momentum[0] * x_sites % extent).astype(jnp.float32) / extent
    y_turns = (momentum[1] * y_sites % LY).astype(jnp.float32) / LY
    z_turns = (momentum[2] * z_sites % LZ).astype(jnp.float32) / LZ
    angles = -2.0 * math.pi * (x_turns[:, None, None] + y_turns[None, :, None] + z_turns[None, None, :])
    angles = angles.reshape(x_sites.shape[0], LY * LZ)
    return (jnp.cos(angles), jnp.sin(angles))

def roll_inner(field_in, axis_pos):
    leading_shape = field_in.shape[:-1]
    grid = field_in.reshape(leading_shape + (LY, LZ))
    grid = jnp.roll(grid, -1, axis=axis_pos)
    return grid.reshape(field_in.shape)

def along_first(vectors):
    return jnp.roll(vectors, -1, axis=3)

def along_second(vectors):
    return roll_inner(vectors, -2)

def along_third(vectors):
    return roll_inner(vectors, -1)

def transport(link_now, source):
    link_re = link_now[0].astype(jnp.float32)
    link_im = link_now[1].astype(jnp.float32)
    src_re = source[0].astype(jnp.float32)
    src_im = source[1].astype(jnp.float32)
    rows_re = []
    rows_im = []
    for row in range(3):
        acc_re = link_re[row, 0] * src_re[0] - link_im[row, 0] * src_im[0]
        acc_im = link_re[row, 0] * src_im[0] + link_im[row, 0] * src_re[0]
        for column in range(1, 3):
            acc_re = acc_re + link_re[row, column] * src_re[column] - link_im[row, column] * src_im[column]
            acc_im = acc_im + link_re[row, column] * src_im[column] + link_im[row, column] * src_re[column]
        rows_re.append(acc_re)
        rows_im.append(acc_im)
    return jnp.stack([jnp.stack(rows_re), jnp.stack(rows_im)]).astype(jnp.bfloat16)

def pair_products(leading, partner, cosine, sine_values):
    lead_re = leading[0].astype(jnp.float32)
    lead_im = leading[1].astype(jnp.float32)
    part_re = partner[0].astype(jnp.float32)
    part_im = partner[1].astype(jnp.float32)
    layers = [None, None, None]
    for one_color, two_color, out_color in epsilon_cycles:
        prod_re = lead_re[one_color][:, None] * part_re[two_color][None] - lead_im[one_color][:, None] * part_im[two_color][None] - lead_re[two_color][:, None] * part_re[one_color][None] + lead_im[two_color][:, None] * part_im[one_color][None]
        prod_im = lead_re[one_color][:, None] * part_im[two_color][None] + lead_im[one_color][:, None] * part_re[two_color][None] - lead_re[two_color][:, None] * part_im[one_color][None] - lead_im[two_color][:, None] * part_re[one_color][None]
        layers[out_color] = (prod_re * cosine - prod_im * sine_values, prod_re * sine_values + prod_im * cosine)
    real_part = jnp.stack([layers[0][0], layers[1][0], layers[2][0]])
    imag_part = jnp.stack([layers[0][1], layers[1][1], layers[2][1]])
    return jnp.stack([real_part, imag_part]).astype(jnp.bfloat16)

def contract(products, vectors):
    flat_products = products.reshape(products.shape[:4] + (-1,)).astype(jnp.float32)
    flat_vectors = vectors.reshape(vectors.shape[:3] + (-1,)).astype(jnp.float32)
    blocks = jnp.einsum('rkabs,qkcs->brqac', flat_products, flat_vectors)
    return jnp.stack([blocks[:, 0, 0] - blocks[:, 1, 1], blocks[:, 0, 1] + blocks[:, 1, 0]], axis=1)

def reference(eigenvectors, link_field, momentum, directions, offsets):
    norm_factor = 1.0 / math.sqrt(LX * LY * LZ)
    cos_all, sin_all = phase_table(momentum, jnp.arange(LX, dtype=jnp.int32), LX)
    results = []
    for tslice in range(TSL):
        vectors = eigenvectors[tslice]
        direction = directions[tslice]
        source = lax.switch(direction, [along_first, along_second, along_third], vectors)
        link_now = lax.dynamic_index_in_dim(link_field[tslice], direction, 0, keepdims=False)
        displaced = transport(link_now, source)
        leading = lax.dynamic_slice_in_dim(vectors, offsets[tslice].astype(jnp.int32), BLK, axis=2)

        def accumulate(running, plane, leading=leading, displaced=displaced, vectors=vectors):

            def take_plane(array, axis_pos):
                return lax.dynamic_slice_in_dim(array, plane, 1, axis=axis_pos)
            products = pair_products(take_plane(leading, 3), take_plane(displaced, 3), take_plane(cos_all, 0), take_plane(sin_all, 0))
            return (running + contract(products, take_plane(vectors, 3)), None)
        running, _ = lax.scan(accumulate, jnp.zeros((NEV, 2, BLK, NEV), jnp.float32), jnp.arange(LX, dtype=jnp.int32))
        results.append(jnp.transpose(running * norm_factor, (1, 2, 0, 3)))
    return jnp.stack(results)
```

```python
import math

import jax
import jax.numpy as jnp
from jax import lax
from jax.experimental import pallas as pl
from jax.experimental.pallas import tpu as pltpu
from jax.sharding import PartitionSpec as P

BLK = 4
LY = 32
LZ = 32
ROWS = 16
LANES = 128

epsilon_cycles = ((0, 1, 2), (1, 2, 0), (2, 0, 1))


def phase_table(momentum, x_site, extent):
    y_sites = jnp.arange(LY, dtype=jnp.int32)
    z_sites = jnp.arange(LZ, dtype=jnp.int32)
    x_turns = (momentum[0] * x_site % extent).astype(jnp.float32) / extent
    y_turns = (momentum[1] * y_sites % LY).astype(jnp.float32) / LY
    z_turns = (momentum[2] * z_sites % LZ).astype(jnp.float32) / LZ
    angles = -2.0 * math.pi * (x_turns + y_turns[:, None] + z_turns[None, :])
    angles = angles.reshape(LY * LZ)
    return jnp.cos(angles), jnp.sin(angles)


def shift_inside(direction, vec_ref, src_ref):
    nev, sites = vec_ref.shape[-2:]

    def fill(shifted):
        def step(block, carry):
            rows = pl.ds(pl.multiple_of(block * ROWS, ROWS), ROWS)
            for part in range(2):
                for color in range(3):
                    values = vec_ref[0, part, color, rows, :].astype(jnp.float32)
                    src_ref[part, color, rows, :] = shifted(values).astype(jnp.bfloat16)
            return carry

        lax.fori_loop(0, nev // ROWS, step, 0)

    def along_third(values):
        lane = lax.broadcasted_iota(jnp.int32, values.shape, 1)
        ahead = pltpu.roll(values, sites - 1, 1)
        wrapped = pltpu.roll(values, LZ - 1, 1)
        return jnp.where(lane % LZ == LZ - 1, wrapped, ahead)

    @pl.when(direction == 1)
    def _():
        fill(lambda values: pltpu.roll(values, sites - LZ, 1))

    @pl.when(direction != 1)
    def _():
        fill(along_third)


def elementals_kernel(shifting, scale, *refs):
    if shifting:
        meta_ref, vec_ref, link_ref, lead_ref, out_ref, prod_ref, rhs_ref, u_ref, src_ref = refs
        shift_inside(meta_ref[1, pl.program_id(0)], vec_ref, src_ref)
    else:
        meta_ref, vec_ref, link_ref, lead_ref, src_ref, out_ref, prod_ref, rhs_ref, u_ref = refs
    nev, sites = vec_ref.shape[-2:]

    for entry in range(9):
        pair = link_ref[0, 0, entry].astype(jnp.float32)
        u_re, u_im = pair[0:1], pair[1:2]
        u_ref[entry : entry + 1, :] = u_re
        u_ref[9 + entry : 10 + entry, :] = u_im - u_re
        u_ref[18 + entry : 19 + entry, :] = u_re + u_im

    for color in range(3):
        vec_re = vec_ref[0, 0, color]
        vec_im = vec_ref[0, 1, color]
        first = slice(color * sites, (color + 1) * sites)
        second = slice((3 + color) * sites, (4 + color) * sites)
        rhs_ref[0:nev, first] = vec_re
        rhs_ref[nev : 2 * nev, first] = vec_im
        rhs_ref[0:nev, second] = -vec_im
        rhs_ref[nev : 2 * nev, second] = vec_re

    def lane_step(lane_block, carry):
        lane = pl.multiple_of(lane_block * LANES, LANES)
        lanes = pl.ds(lane, LANES)

        def row(ref, index):
            return jnp.broadcast_to(ref[pl.ds(index, 1), lanes], (ROWS, LANES))

        def lead_row(index):
            return jnp.broadcast_to(lead_ref[0, pl.ds(index, 1), lanes], (ROWS, LANES))

        def row_step(block, carry):
            rows = pl.ds(pl.multiple_of(block * ROWS, ROWS), ROWS)
            s_re = [src_ref[0, j, rows, lanes].astype(jnp.float32) for j in range(3)]
            s_im = [src_ref[1, j, rows, lanes].astype(jnp.float32) for j in range(3)]
            s_sum = [s_re[j] + s_im[j] for j in range(3)]
            d_re, d_im, d_sum = [], [], []
            for i in range(3):
                k1 = k2 = k3 = None
                for j in range(3):
                    entry = 3 * i + j
                    t1 = row(u_ref, entry) * s_sum[j]
                    t2 = row(u_ref, 9 + entry) * s_re[j]
                    t3 = row(u_ref, 18 + entry) * s_im[j]
                    k1 = t1 if k1 is None else k1 + t1
                    k2 = t2 if k2 is None else k2 + t2
                    k3 = t3 if k3 is None else k3 + t3
                re = (k1 - k3).astype(jnp.bfloat16).astype(jnp.float32)
                im = (k1 + k2).astype(jnp.bfloat16).astype(jnp.float32)
                d_re.append(re)
                d_im.append(im)
                d_sum.append(re + im)
            for a in range(BLK):
                out_rows = pl.ds(pl.multiple_of(block * ROWS + a * nev, ROWS), ROWS)
                for i, j, k in epsilon_cycles:
                    at_i, at_j = 3 * a + i, 3 * a + j
                    k1 = lead_row(at_i) * d_sum[j] - lead_row(at_j) * d_sum[i]
                    k2 = lead_row(12 + at_i) * d_re[j] - lead_row(12 + at_j) * d_re[i]
                    k3 = lead_row(24 + at_i) * d_im[j] - lead_row(24 + at_j) * d_im[i]
                    first = pl.ds(pl.multiple_of(lane + k * sites, LANES), LANES)
                    second = pl.ds(pl.multiple_of(lane + (3 + k) * sites, LANES), LANES)
                    prod_ref[out_rows, first] = (k1 - k3).astype(jnp.bfloat16)
                    prod_ref[out_rows, second] = (k1 + k2).astype(jnp.bfloat16)
            return carry

        return lax.fori_loop(0, nev // ROWS, row_step, carry)

    lax.fori_loop(0, sites // LANES, lane_step, 0)

    sums = lax.dot_general(
        prod_ref[...],
        rhs_ref[...],
        (((1,), (1,)), ((), ())),
        preferred_element_type=jnp.float32,
    )
    sums = sums * scale
    for part in range(2):
        for a in range(BLK):
            block = sums[a * nev : (a + 1) * nev, part * nev : (part + 1) * nev]
            out_ref[0, part * BLK + a] = block.astype(jnp.bfloat16)


def elementals_call(shifting, scale, meta, vectors, links, leads, source=None):
    count = meta.shape[1]
    _, _, _, nev, sites = vectors.shape
    in_specs = [
        pl.BlockSpec((1, 2, 3, nev, sites), lambda n, meta: (meta[0, n], 0, 0, 0, 0)),
        pl.BlockSpec((1, 1, 9, 2, sites), lambda n, meta: (meta[0, n], meta[1, n], 0, 0, 0)),
        pl.BlockSpec((1, 9 * BLK, sites), lambda n, meta: (meta[0, n], 0, 0)),
    ]
    operands = [meta, vectors, links, leads]
    scratch = [
        pltpu.VMEM((BLK * nev, 6 * sites), jnp.bfloat16),
        pltpu.VMEM((2 * nev, 6 * sites), jnp.bfloat16),
        pltpu.VMEM((32, sites), jnp.float32),
    ]
    if shifting:
        scratch.append(pltpu.VMEM((2, 3, nev, sites), jnp.bfloat16))
    else:
        in_specs.append(pl.BlockSpec((2, 3, nev, sites), lambda n, meta: (0, 0, 0, 0)))
        operands.append(source)

    def body(*refs):
        elementals_kernel(shifting, scale, *refs)

    return pl.pallas_call(
        body,
        out_shape=jax.ShapeDtypeStruct((count, 2 * BLK, nev, nev), jnp.bfloat16),
        grid_spec=pltpu.PrefetchScalarGridSpec(
            num_scalar_prefetch=1,
            grid=(count,),
            in_specs=in_specs,
            out_specs=pl.BlockSpec((1, 2 * BLK, nev, nev), lambda n, meta: (n, 0, 0, 0)),
            scratch_shapes=scratch,
        ),
        compiler_params=pltpu.CompilerParams(
            dimension_semantics=("arbitrary",), vmem_limit_bytes=48 * 1024 * 1024
        ),
        cost_estimate=pl.CostEstimate(
            flops=count * 16 * BLK * 3 * nev * nev * sites,
            bytes_accessed=count * 16 * 3 * nev * sites,
            transcendentals=0,
        ),
        name="shift_elementals" if shifting else "halo_elementals",
    )(*operands)


def on_device(eigenvectors, link_field, momentum, directions, offsets):
    devices = lax.axis_size("space")
    tsl, _, _, nev, planes, sites = eigenvectors.shape
    assert planes == 1
    extent_x = planes * devices
    scale = 1.0 / math.sqrt(extent_x * sites)
    vectors = eigenvectors.reshape(tsl, 2, 3, nev, sites)
    links = jnp.transpose(link_field, (0, 1, 3, 4, 5, 2, 6)).reshape(tsl, 3, 9, 2, sites)

    order = jnp.argsort(jnp.where(directions == 0, 1, 0), stable=True).astype(jnp.int32)
    meta = jnp.stack([order, directions[order]])
    half = tsl // 2

    pairs = [(device, (device - 1) % devices) for device in range(devices)]
    halos = [
        lax.ppermute(
            lax.dynamic_index_in_dim(vectors, order[half + n], 0, keepdims=False), "space", pairs
        )
        for n in range(half)
    ]

    cosine, sine = phase_table(momentum, lax.axis_index("space"), extent_x)
    lead = jnp.stack(
        [lax.dynamic_slice_in_dim(vectors[t], offsets[t], BLK, axis=2) for t in range(tsl)]
    ).astype(jnp.float32)
    lead = jnp.swapaxes(lead, 2, 3)
    lead_re = lead[:, 0] * cosine - lead[:, 1] * sine
    lead_im = lead[:, 0] * sine + lead[:, 1] * cosine
    leads = jnp.stack([lead_re, lead_im - lead_re, lead_re + lead_im], axis=1)
    leads = leads.reshape(tsl, 9 * BLK, sites)

    def spread(partial):
        count = partial.shape[0]
        parts = partial.reshape(count, 2 * BLK, devices, nev // devices, nev)
        parts = jnp.moveaxis(parts, 2, 0)
        parts = lax.all_to_all(parts, "space", 0, 0, tiled=True)
        return jnp.sum(parts.astype(jnp.float32), axis=0)

    partials = [elementals_call(True, scale, meta[:, :half], vectors, links, leads)]
    for n in range(half):
        where = meta[:, half + n : half + n + 1]
        partials.append(elementals_call(False, scale, where, vectors, links, leads, halos[n]))
    early = spread(jnp.concatenate(partials[:-1]))
    late = spread(partials[-1])
    sums = jnp.concatenate([early, late])
    back = jnp.argsort(order)
    sums = jnp.take(sums, back, axis=0)
    return sums.reshape(tsl, 2, BLK, nev // devices, nev)


def solution(mesh):
    placed = (
        P("cfg", None, None, None, "space", None),
        P("cfg", None, None, None, None, "space", None),
        P(),
        P(),
        P(),
    )
    return jax.shard_map(
        on_device,
        mesh=mesh,
        in_specs=placed,
        out_specs=P("cfg", None, None, "space", None),
        check_vma=False,
    )
```

```python
import functools
import math

import jax
import jax.numpy as jnp
from jax import lax
from jax.experimental import pallas as pl
from jax.experimental.pallas import tpu as pltpu
from jax.sharding import PartitionSpec as P

BLK = 4
LY = 32
LZ = 32
SUB = 8
LANES = 128
MIB = 1024 * 1024

epsilon_cycles = ((0, 1, 2), (1, 2, 0), (2, 0, 1))


def nth_slice(dir_ref, tsl, zero, last):
    index = jnp.int32(0)
    for t in range(tsl) if last else reversed(range(tsl)):
        index = jnp.where((dir_ref[t] == 0) == zero, jnp.int32(t), index)
    return index


def floor_mod(value, extent):
    if extent & (extent - 1) == 0:
        return value & (extent - 1)
    return jnp.remainder(value, extent)


def copy_kernel(dir_ref, in_ref, out_ref):
    out_ref[...] = in_ref[0]


def plane_to_send(directions, vectors, last):
    tsl, _, _, nev, sites = vectors.shape
    return pl.pallas_call(
        copy_kernel,
        out_shape=jax.ShapeDtypeStruct((2, 3, nev, sites), vectors.dtype),
        grid_spec=pltpu.PrefetchScalarGridSpec(
            num_scalar_prefetch=1,
            grid=(2, 3),
            in_specs=[
                pl.BlockSpec(
                    (1, 1, 1, nev, sites),
                    lambda r, k, d: (nth_slice(d, tsl, True, last), r, k, 0, 0),
                )
            ],
            out_specs=pl.BlockSpec((1, 1, nev, sites), lambda r, k, d: (r, k, 0, 0)),
        ),
        name="plane_to_send",
    )(directions, vectors)


def shift_inside(direction, vec_ref, src_ref):
    nev, sites = vec_ref.shape[-2:]
    rows_step = 2 * SUB

    def fill(shifted):
        def step(block, carry):
            rows = pl.ds(pl.multiple_of(block * rows_step, rows_step), rows_step)
            for part in range(2):
                for color in range(3):
                    values = vec_ref[0, part, color, rows, :].astype(jnp.float32)
                    src_ref[part, color, rows, :] = shifted(values).astype(jnp.bfloat16)
            return carry

        lax.fori_loop(0, nev // rows_step, step, 0)

    def along_third(values):
        lane = lax.broadcasted_iota(jnp.int32, values.shape, 1)
        ahead = pltpu.roll(values, sites - 1, 1)
        wrapped = pltpu.roll(values, LZ - 1, 1)
        return jnp.where(lane % LZ == LZ - 1, wrapped, ahead)

    @pl.when(direction == 1)
    def _():
        fill(lambda values: pltpu.roll(values, sites - LZ, 1))

    @pl.when(direction != 1)
    def _():
        fill(along_third)


def phase_rows(mom_ref, extent, sites):
    shape = (SUB, sites)
    site = lax.broadcasted_iota(jnp.int32, shape, 1)
    x_site = lax.axis_index("space")
    x_part = floor_mod(jnp.full(shape, mom_ref[0] * x_site, jnp.int32), extent)
    y_part = floor_mod(mom_ref[1] * (site // LZ), LY)
    z_part = floor_mod(mom_ref[2] * (site % LZ), LZ)
    turns = (
        x_part.astype(jnp.float32) / extent
        + y_part.astype(jnp.float32) / LY
        + z_part.astype(jnp.float32) / LZ
    )
    angles = -2.0 * math.pi * turns
    return jnp.cos(angles), jnp.sin(angles)


def elementals_kernel(shifting, extent, scale, tsl, *refs):
    dir_ref, off_ref, mom_ref, vec_ref, link_ref = refs[:5]
    if shifting:
        out_ref, prod_ref, rhs_ref, acc_ref, u_ref, lead_ref, src_ref = refs[5:]
        which = pl.program_id(0)
        t = jnp.where(
            which == 0, nth_slice(dir_ref, tsl, False, False), nth_slice(dir_ref, tsl, False, True)
        )
        shift_inside(dir_ref[t], vec_ref, src_ref)
    else:
        src_ref, _, out_ref, prod_ref, rhs_ref, acc_ref, u_ref, lead_ref = refs[5:]
        t = nth_slice(dir_ref, tsl, True, shifting is None)
    nev, sites = vec_ref.shape[-2:]
    half = nev // 2
    blocks = sites // LANES

    for entry in range(9):
        pair = link_ref[0, 0, entry].astype(jnp.float32)
        u_re, u_im = pair[0:1], pair[1:2]
        u_ref[entry : entry + 1, :] = u_re
        u_ref[9 + entry : 10 + entry, :] = u_im - u_re
        u_ref[18 + entry : 19 + entry, :] = u_re + u_im

    cosine, sine = phase_rows(mom_ref, extent, sites)
    row_id = lax.broadcasted_iota(jnp.int32, (SUB, nev), 0)
    col_id = lax.broadcasted_iota(jnp.int32, (SUB, nev), 1)
    chosen = jnp.where(col_id == row_id + off_ref[t], 1.0, 0.0).astype(jnp.bfloat16)
    for color in range(3):
        raw_re = jnp.dot(chosen, vec_ref[0, 0, color], preferred_element_type=jnp.float32)
        raw_im = jnp.dot(chosen, vec_ref[0, 1, color], preferred_element_type=jnp.float32)
        lead_re = raw_re * cosine - raw_im * sine
        lead_im = raw_re * sine + raw_im * cosine
        lead_ref[color * SUB : (color + 1) * SUB, :] = lead_re
        lead_ref[(3 + color) * SUB : (4 + color) * SUB, :] = lead_im - lead_re
        lead_ref[(6 + color) * SUB : (7 + color) * SUB, :] = lead_re + lead_im

    for color in range(3):
        for block in range(blocks):
            lanes = slice(block * LANES, (block + 1) * LANES)
            vec_re = vec_ref[0, 0, color, :, lanes]
            vec_im = vec_ref[0, 1, color, :, lanes]
            first = slice(2 * color * LANES, (2 * color + 1) * LANES)
            second = slice((2 * color + 1) * LANES, (2 * color + 2) * LANES)
            rhs_ref[block, 0:nev, first] = vec_re
            rhs_ref[block, nev : 2 * nev, first] = vec_im
            rhs_ref[block, 0:nev, second] = -vec_im
            rhs_ref[block, nev : 2 * nev, second] = vec_re

    acc_ref[...] = jnp.zeros_like(acc_ref)
    prod_ref[1] = jnp.zeros_like(prod_ref[1])

    def vector_part(lane, which):
        lanes = pl.ds(lane, LANES)

        def row(ref, index):
            return jnp.broadcast_to(ref[pl.ds(index, 1), lanes], (SUB, LANES))

        for block in range(half // SUB):
            rows = slice(which * half + block * SUB, which * half + (block + 1) * SUB)
            s_re = [src_ref[0, j, rows, lanes].astype(jnp.float32) for j in range(3)]
            s_im = [src_ref[1, j, rows, lanes].astype(jnp.float32) for j in range(3)]
            s_sum = [s_re[j] + s_im[j] for j in range(3)]
            d_re, d_im, d_sum = [], [], []
            for i in range(3):
                k1 = k2 = k3 = None
                for j in range(3):
                    entry = 3 * i + j
                    t1 = row(u_ref, entry) * s_sum[j]
                    t2 = row(u_ref, 9 + entry) * s_re[j]
                    t3 = row(u_ref, 18 + entry) * s_im[j]
                    k1 = t1 if k1 is None else k1 + t1
                    k2 = t2 if k2 is None else k2 + t2
                    k3 = t3 if k3 is None else k3 + t3
                re = (k1 - k3).astype(jnp.bfloat16).astype(jnp.float32)
                im = (k1 + k2).astype(jnp.bfloat16).astype(jnp.float32)
                d_re.append(re)
                d_im.append(im)
                d_sum.append(re + im)
            for a in range(BLK):
                out_rows = slice(a * half + block * SUB, a * half + (block + 1) * SUB)
                for i, j, k in epsilon_cycles:
                    at_i, at_j = i * SUB + a, j * SUB + a
                    k1 = row(lead_ref, at_i) * d_sum[j] - row(lead_ref, at_j) * d_sum[i]
                    at_i, at_j = at_i + 3 * SUB, at_j + 3 * SUB
                    k2 = row(lead_ref, at_i) * d_re[j] - row(lead_ref, at_j) * d_re[i]
                    at_i, at_j = at_i + 3 * SUB, at_j + 3 * SUB
                    k3 = row(lead_ref, at_i) * d_im[j] - row(lead_ref, at_j) * d_im[i]
                    first = slice(2 * k * LANES, (2 * k + 1) * LANES)
                    second = slice((2 * k + 1) * LANES, (2 * k + 2) * LANES)
                    prod_ref[which, out_rows, first] = (k1 - k3).astype(jnp.bfloat16)
                    prod_ref[which, out_rows, second] = (k1 + k2).astype(jnp.bfloat16)

    def matrix_part(block, which):
        acc_ref[which] += lax.dot_general(
            prod_ref[which],
            rhs_ref[block],
            (((1,), (1,)), ((), ())),
            preferred_element_type=jnp.float32,
        )

    def lane_step(block, carry):
        lane = pl.multiple_of(block * LANES, LANES)
        matrix_part(jnp.maximum(block - 1, 0), 1)
        vector_part(lane, 0)
        matrix_part(block, 0)
        vector_part(lane, 1)
        return carry

    lax.fori_loop(0, blocks, lane_step, 0)
    matrix_part(blocks - 1, 1)

    for which in range(2):
        for a in range(BLK):
            for part in range(2):
                block = acc_ref[
                    which, a * half : (a + 1) * half, part * nev : (part + 1) * nev
                ]
                block = (block * scale).astype(jnp.bfloat16)
                where = part * BLK + a
                if len(out_ref.shape) == 5:
                    count = half // SUB
                    out_ref[which * count : (which + 1) * count, 0, where] = block.reshape(
                        count, SUB, nev
                    )
                else:
                    out_ref[0, where, which * half : (which + 1) * half] = block


def elementals_call(kind, place, total, extent, scale, scalars, vectors, links, source, into, tiled):
    shifting = kind == "inside"
    last = kind == "last"
    tsl, _, _, nev, sites = vectors.shape
    count = 2 if shifting else 1

    def index_of(n, d):
        if shifting:
            first = nth_slice(d, tsl, False, False)
            return jnp.where(n == 0, first, nth_slice(d, tsl, False, True))
        return nth_slice(d, tsl, True, last)

    in_specs = [
        pl.BlockSpec((1, 2, 3, nev, sites), lambda n, d, o, m: (index_of(n, d), 0, 0, 0, 0)),
        pl.BlockSpec(
            (1, 1, 9, 2, sites), lambda n, d, o, m: (index_of(n, d), d[index_of(n, d)], 0, 0, 0)
        ),
    ]
    operands = [*scalars, vectors, links]
    scratch = [
        pltpu.VMEM((2, BLK * nev // 2, 6 * LANES), jnp.bfloat16),
        pltpu.VMEM((sites // LANES, 2 * nev, 6 * LANES), jnp.bfloat16),
        pltpu.VMEM((2, BLK * nev // 2, 2 * nev), jnp.float32),
        pltpu.VMEM((32, sites), jnp.float32),
        pltpu.VMEM((9 * SUB, sites), jnp.float32),
    ]
    aliases = {}
    if shifting:
        scratch.append(pltpu.VMEM((2, 3, nev, sites), jnp.bfloat16))
    else:
        in_specs.append(pl.BlockSpec((2, 3, nev, sites), lambda n, d, o, m: (0, 0, 0, 0)))
        in_specs.append(pl.BlockSpec(memory_space=pl.ANY))
        operands += [source, into]
        if total > 1:
            aliases = {len(operands) - 1: 0}
    if tiled:
        shape = (nev // SUB, total, 2 * BLK, SUB, nev)
        block = (nev // SUB, 1, 2 * BLK, SUB, nev)
        out_spec = pl.BlockSpec(block, lambda n, d, o, m: (0, place + n, 0, 0, 0))
    else:
        shape = (total, 2 * BLK, nev, nev)
        block = (1, 2 * BLK, nev, nev)
        out_spec = pl.BlockSpec(block, lambda n, d, o, m: (place + n, 0, 0, 0))

    mode = True if shifting else (None if last else False)
    return pl.pallas_call(
        functools.partial(elementals_kernel, mode, extent, scale, tsl),
        out_shape=jax.ShapeDtypeStruct(shape, jnp.bfloat16),
        grid_spec=pltpu.PrefetchScalarGridSpec(
            num_scalar_prefetch=3,
            grid=(count,),
            in_specs=in_specs,
            out_specs=out_spec,
            scratch_shapes=scratch,
        ),
        input_output_aliases=aliases,
        compiler_params=pltpu.CompilerParams(
            dimension_semantics=("arbitrary",), vmem_limit_bytes=40 * MIB
        ),
        cost_estimate=pl.CostEstimate(
            flops=count * 16 * BLK * 3 * nev * nev * sites,
            bytes_accessed=count * 16 * 3 * nev * sites,
            transcendentals=0,
        ),
        name=kind + "_elementals",
    )(*operands)


def sum_kernel(first, *refs):
    in_ref, out_ref = refs[1], refs[-1]
    total = in_ref[0, 0].astype(jnp.float32)
    for device in range(1, in_ref.shape[0]):
        total = total + in_ref[device, 0].astype(jnp.float32)
    out_ref[0] = total


def sum_parts(directions, parts, first, tsl, into):
    devices, count = parts.shape[:2]
    body = parts.shape[2:]
    zeros = (0,) * len(body)

    def index_of(n, d):
        if not first:
            return nth_slice(d, tsl, True, True)
        one = nth_slice(d, tsl, False, False)
        two = nth_slice(d, tsl, False, True)
        return jnp.where(n == 0, one, jnp.where(n == 1, two, nth_slice(d, tsl, True, False)))

    in_specs = [pl.BlockSpec((devices, 1) + body, lambda n, d: (0, n) + zeros)]
    operands = [directions, parts]
    if not first:
        in_specs.append(pl.BlockSpec(memory_space=pl.ANY))
        operands.append(into)
    return pl.pallas_call(
        functools.partial(sum_kernel, first),
        out_shape=jax.ShapeDtypeStruct((tsl,) + body, jnp.float32),
        grid_spec=pltpu.PrefetchScalarGridSpec(
            num_scalar_prefetch=1,
            grid=(count,),
            in_specs=in_specs,
            out_specs=pl.BlockSpec((1,) + body, lambda n, d: (index_of(n, d),) + zeros),
        ),
        input_output_aliases={} if first else {2: 0},
        name="sum_parts",
    )(*operands)


def on_device(eigenvectors, link_field, momentum, directions, offsets):
    devices = lax.axis_size("space")
    tsl, _, _, nev, planes, sites = eigenvectors.shape
    assert planes == 1 and tsl == 4
    extent = planes * devices
    scale = 1.0 / math.sqrt(extent * sites)
    vectors = eigenvectors.reshape(tsl, 2, 3, nev, sites)
    links = jnp.transpose(link_field, (0, 1, 3, 4, 5, 2, 6)).reshape(tsl, 3, 9, 2, sites)
    tiled = nev // devices == SUB

    pairs = [(device, (device - 1) % devices) for device in range(devices)]
    halos = [
        lax.ppermute(plane_to_send(directions, vectors, last), "space", pairs)
        for last in (False, True)
    ]

    scalars = (directions, offsets, momentum)
    call = functools.partial(
        elementals_call,
        extent=extent,
        scale=scale,
        scalars=scalars,
        vectors=vectors,
        links=links,
        tiled=tiled,
    )
    early = call("inside", 0, 3, source=None, into=None)
    early = call("first", 2, 3, source=halos[0], into=early)
    late = call("last", 0, 1, source=halos[1], into=early)

    def exchange(partial):
        if not tiled:
            count = partial.shape[0]
            partial = partial.reshape(count, 2 * BLK, devices, nev // devices, nev)
            partial = jnp.moveaxis(partial, 2, 0)
        return lax.all_to_all(partial, "space", 0, 0, tiled=True)

    sums = sum_parts(directions, exchange(early), True, tsl, None)
    sums = sum_parts(directions, exchange(late), False, tsl, sums)
    return sums.reshape(tsl, 2, BLK, nev // devices, nev)


def solution(mesh):
    placed = (
        P("cfg", None, None, None, "space", None),
        P("cfg", None, None, None, None, "space", None),
        P(),
        P(),
        P(),
    )
    return jax.shard_map(
        on_device,
        mesh=mesh,
        in_specs=placed,
        out_specs=P("cfg", None, None, "space", None),
        check_vma=False,
    )
```
